256 devices in a mesh: req: 32 (over z, y_lo, core), ctx: 8 (over x, y_hi).
Axes of the slice: x: 4, y: 4 (y_hi: 2, y_lo: 2; y = y_hi * 2 + y_lo), z: 8, core: 2. Of those that a mesh axis runs over, the one named last changes fastest.
Arguments:
- queries: bfloat16 [32, 128, 4096], P('req', 'ctx'), may hold values from -6 to 6
- fresh_kv: bfloat16 [32, 128, 1024], P('req', 'ctx'), may hold values from -6 to 6
- cache_pages: bfloat16 [32, 8, 32, 64, 1024], P('req', 'ctx'), may hold values from -400 to 400
- stretch_store: int32 [32, 8, 32], P('req', 'ctx'), may hold values from 0 to 31, as said below
- stretch_request: int32 [32, 8, 32], P('req', 'ctx'), may hold values from 0 to 31, as said below
- recompute_idx: int32 [32, 8, 16], P('req'), may hold values from 0 to 2047, as said below
- block_mask: int32 [32, 8, 2, 8, 32], P('req'), may hold values 0 or 1
Outputs:
- attended: bfloat16 [32, 128, 4096], P('req', 'ctx')
- joined_cache: bfloat16 [32, 16384, 1024], P('req', 'ctx')
The draws below stay inside these ranges and needn't reach their ends.
Inputs may be any that keep to these rules, and one draw needn't show every extreme that they name: The page at position j of request r's shard on ctx index c lies on store stretch_store[r, c, j] of the same ctx index; the 32 pages of one shard lie on 32 different stores. `stretch_request`: A store's 32 slots belong to 32 different requests, and for each entry of stretch_store exactly one slot of the named store names that request. `recompute_idx`: within a shard the indices are distinct and increasing and include 0 and 2047.
All inputs are finite; a program needn't handle non-finite values. No bound on the sum of `block_mask` on one device may be relied on, other than what follows from the above.
Results may differ from the reference program's by a relative error of at most 0.02.
The reference program's roundings to bfloat16 on the way count: a program that leaves them out, or rounds other values in their place, can miss the bound.
Values may be sent and summed in bfloat16 or wider, within the bound.
No kernel may reach another device: no remote copies, remote signals or barrier semaphores. Data moves between devices by JAX's collectives and lax.ppermute only.
A program may use at most 64 MiB of HBM per device.

```python
import math
import jax
import jax.numpy as jnp
from jax import lax

QHEADS = 32
KVHEADS = 4
HEAD = 128
PAGE = 64
TILE = 8
RECOMP = 16
REQS = 32
PAGES = 32
SHARDS = 8
TILES = 2


def stretch_tables(key):
    base_key = jax.random.fold_in(key, 29)

    def column(column_key):
        four_keys = jax.random.split(column_key, 4)
        store_perm = jax.random.permutation(four_keys[0], REQS)
        owner_perm = jax.random.permutation(four_keys[1], REQS)
        shifts = jax.random.permutation(four_keys[2], REQS)[:PAGES]
        store_inverse = jnp.argsort(store_perm, stable=True)
        owner_inverse = jnp.argsort(owner_perm, stable=True)
        owners = owner_inverse[(store_perm[:, None] - shifts[None, :]) % REQS]
        homes = store_inverse[(owner_perm[:, None] + shifts[None, :]) % REQS]
        orders = jax.vmap(lambda order_key: jax.random.permutation(order_key, PAGES))(jax.random.split(four_keys[3], REQS))
        placed = jnp.take_along_axis(homes, orders, axis=1)
        return (placed.astype(jnp.int32), owners.astype(jnp.int32))
    placed, owners = jax.vmap(column)(jax.random.split(base_key, SHARDS))
    return (jnp.transpose(placed, (1, 0, 2)), jnp.transpose(owners, (1, 0, 2)))


def draw_stretch_store(key, part):
    return stretch_tables(key)[0]


def draw_stretch_request(key, part):
    return stretch_tables(key)[1]


def draw_recompute_idx(key, part):
    span_len = PAGES * PAGE

    def choose_rows(pick_key):
        middle_rows = jax.random.permutation(pick_key, span_len - 2)[:RECOMP - 2] + 1
        chosen_rows = jnp.concatenate([jnp.array([0, span_len - 1], dtype=jnp.int32), middle_rows.astype(jnp.int32)])
        return jnp.sort(chosen_rows)
    row_keys = jax.random.split(jax.random.fold_in(key, 31), REQS * SHARDS)
    return jax.vmap(choose_rows)(row_keys).reshape(REQS, SHARDS, RECOMP)


def draw_cache_pages(key, part):
    feature = KVHEADS * HEAD
    shape = (REQS, SHARDS, PAGES, PAGE, 2 * feature)
    three_keys = jax.random.split(jax.random.fold_in(key, 11), 1)
    values = jnp.clip(jax.random.normal(three_keys[0], shape, jnp.float32), -6.0, 6.0)
    return values.astype(jnp.bfloat16)


def set_ends(values, own_key, least, high):
    shape = values.shape
    index_at = [jax.random.randint(jax.random.fold_in(own_key, axis), (), 0, shape[axis]) for axis in range(len(shape))]
    values = values.at[tuple(index_at)].set(least)
    longest = shape.index(max(shape))
    index_at[longest] = (index_at[longest] + 1) % shape[longest]
    return values.at[tuple(index_at)].set(high)


def levels(own_key, extent, shards, smallest, largest):
    def one(dim, blocks):
        heights = jax.random.uniform(jax.random.fold_in(jax.random.fold_in(own_key, 6), dim), (blocks,), jnp.float32, smallest / len(shards), largest / len(shards))
        return jnp.repeat(jnp.exp(heights), extent[dim] // blocks).reshape((-1,) + (1,) * (len(extent) - dim - 1))

    factor_of = one(*shards[0])
    for cut in shards[1:]:
        factor_of = factor_of * one(*cut)
    return factor_of


def normal_values(own_key, shape, spread, reach, cuts=(), held_as=jnp.bfloat16):
    drawn = jax.random.normal(own_key, shape, jnp.float32) * spread
    if len(cuts) > 0:
        drawn = levels(own_key, shape, cuts, -0.22, 0.18) * drawn
    return jnp.clip(drawn, min=-reach, max=reach).astype(held_as)


def setup_inputs(seed: int = 0) -> dict:
    splits = jax.random.split(jax.random.key(seed), 8)
    return {
        "queries": normal_values(splits[0], (REQS, SHARDS * RECOMP, QHEADS * HEAD), 1.0, 6.0, ((0, 32), (1, 8))),
        "fresh_kv": normal_values(splits[1], (REQS, SHARDS * RECOMP, 2 * KVHEADS * HEAD), 1.0, 6.0, ((0, 32), (1, 8))),
        "cache_pages": draw_cache_pages(jax.random.fold_in(splits[7], 71), 0),
        "stretch_store": draw_stretch_store(jax.random.fold_in(splits[7], 71), 0),
        "stretch_request": draw_stretch_request(jax.random.fold_in(splits[7], 71), 0),
        "recompute_idx": draw_recompute_idx(jax.random.fold_in(splits[7], 71), 0),
        "block_mask": set_ends((jax.random.randint(splits[6], (REQS, SHARDS, TILES, SHARDS, PAGES), 0, 2) < 1).astype(jnp.int32), jax.random.fold_in(splits[6], 1), 0, 1),
    }


THETA = 500000.0
NEG = -1e+30

def rotary(values, position, head_count):
    number = values.shape[0]
    half_size = HEAD // 2
    frequency = jnp.exp(-(2.0 * jnp.arange(half_size, dtype=jnp.float32) / HEAD) * math.log(THETA))
    angles = position.astype(jnp.float32)[:, None] * frequency[None, :]
    cosine = jnp.cos(angles)[:, None, :]
    sine = jnp.sin(angles)[:, None, :]
    shaped = values.astype(jnp.float32).reshape(number, head_count, HEAD)
    first_half = shaped[..., :half_size]
    second_half = shaped[..., half_size:]
    turned = jnp.concatenate([first_half * cosine - second_half * sine, second_half * cosine + first_half * sine], axis=-1)
    return turned.reshape(number, head_count * HEAD)

def reference(queries, fresh_kv, cache_pages, stretch_store, stretch_request, recompute_idx, block_mask):
    feature = KVHEADS * HEAD
    groups = QHEADS // KVHEADS
    span_len = PAGES * PAGE
    total_len = SHARDS * span_len

    def assemble(request, shard_index):
        sources = stretch_store[request, shard_index]
        owners = stretch_request[sources, shard_index]
        chosen = (owners == request).astype(jnp.float32)
        summed = jnp.zeros((PAGES, PAGE, 2 * feature), jnp.float32)
        for slot_index in range(PAGES):
            summed = summed + chosen[:, slot_index, None, None] * cache_pages[sources, shard_index, slot_index].astype(jnp.float32)
        return summed.astype(jnp.bfloat16).reshape(span_len, 2 * feature)

    def one_request(request):

        def join(shard_index):
            assembled = assemble(request, shard_index)
            local_rows = recompute_idx[request, shard_index]
            position = shard_index * span_len + local_rows
            fresh_rows = lax.dynamic_slice_in_dim(fresh_kv[request], shard_index * RECOMP, RECOMP, 0)
            turned = rotary(fresh_rows[:, :feature], position, KVHEADS)
            new_rows = jnp.concatenate([turned, fresh_rows[:, feature:].astype(jnp.float32)], axis=1).astype(jnp.bfloat16)
            return assembled.at[local_rows].set(new_rows)
        joined_rows = lax.map(join, jnp.arange(SHARDS, dtype=jnp.int32)).reshape(total_len, 2 * feature)
        key_rows = joined_rows[:, :feature].astype(jnp.float32).reshape(total_len, KVHEADS, HEAD)
        value_rows = joined_rows[:, feature:].astype(jnp.float32).reshape(total_len, KVHEADS, HEAD)
        key_pos = jnp.arange(total_len, dtype=jnp.int32)

        def attend(shard_index):
            position = shard_index * span_len + recompute_idx[request, shard_index]
            raw_rows = lax.dynamic_slice_in_dim(queries[request], shard_index * RECOMP, RECOMP, 0)
            turned = lax.optimization_barrier(rotary(raw_rows, position, QHEADS).astype(jnp.bfloat16)).astype(jnp.float32)
            query_rows = turned.reshape(RECOMP, KVHEADS, groups, HEAD)
            scores = jnp.einsum('rkgd,pkd->kgrp', query_rows, key_rows) / math.sqrt(HEAD)
            tile_mask = block_mask[request, shard_index].reshape(RECOMP // TILE, SHARDS * PAGES)
            per_key = jnp.repeat(jnp.repeat(tile_mask, PAGE, axis=1), TILE, axis=0) == 1
            causal = key_pos[None, :] <= position[:, None]
            same_page = (key_pos // PAGE)[None, :] == (position // PAGE)[:, None]
            allowed = causal & (same_page | per_key)
            masked = jnp.where(allowed, scores, NEG)
            row_max = lax.optimization_barrier(jnp.max(masked, axis=-1, keepdims=True))
            weights = jnp.where(allowed, jnp.exp(masked - row_max), 0.0)
            row_total = lax.optimization_barrier(jnp.sum(weights, axis=-1))
            rounded = lax.optimization_barrier(weights.astype(jnp.bfloat16)).astype(jnp.float32)
            mixture = jnp.einsum('kgrp,pkd->rkgd', rounded, value_rows)
            mixture = mixture / jnp.transpose(row_total, (2, 0, 1))[..., None]
            return mixture.reshape(RECOMP, QHEADS * HEAD).astype(jnp.bfloat16)
        attended = lax.map(attend, jnp.arange(SHARDS, dtype=jnp.int32)).reshape(SHARDS * RECOMP, QHEADS * HEAD)
        return (attended, joined_rows)
    attended, joined_cache = lax.map(one_request, jnp.arange(REQS, dtype=jnp.int32))
    return (attended, joined_cache)
```

```python
import functools
import math

import jax
import jax.numpy as jnp
from jax import lax
from jax.experimental import pallas as pl
from jax.experimental.pallas import tpu as pltpu
from jax.sharding import PartitionSpec as P

QHEADS = 32
KVHEADS = 4
HEAD = 128
TILE = 8
GROUPS = QHEADS // KVHEADS
FEATURE = KVHEADS * HEAD
THETA = 500000.0
NEG = -1e30
FLOOR = -1e6
SCALE = math.log2(math.e) / math.sqrt(HEAD)
LANES = 128
WIDE = GROUPS * HEAD
CHUNKS = ((0, 3), (3, 1))
ANY = pl.BlockSpec(memory_space=pl.ANY)
VMEM = pl.BlockSpec(memory_space=pltpu.VMEM)
SMEM = pl.BlockSpec(memory_space=pltpu.SMEM)


def rotary(values, position, head_count):
    number = values.shape[0]
    half_size = HEAD // 2
    frequency = jnp.exp(-(2.0 * jnp.arange(half_size, dtype=jnp.float32) / HEAD) * math.log(THETA))
    angles = position.astype(jnp.float32)[:, None] * frequency[None, :]
    cosine = jnp.cos(angles)[:, None, :]
    sine = jnp.sin(angles)[:, None, :]
    shaped = values.astype(jnp.float32).reshape(number, head_count, HEAD)
    first_half = shaped[..., :half_size]
    second_half = shaped[..., half_size:]
    turned = jnp.concatenate(
        [first_half * cosine - second_half * sine, second_half * cosine + first_half * sine],
        axis=-1,
    )
    return turned.reshape(number, head_count * HEAD)


def pack_kernel(slot_ref, pages_ref, *refs):
    count = len(CHUNKS)
    outs, held, in_sem, out_sem = refs[:count], refs[count], refs[count + 1], refs[count + 2]
    pages = pages_ref.shape[0]
    load = pltpu.make_async_copy(pages_ref, held, in_sem)
    load.start()
    load.wait()
    for number, (start, heads) in enumerate(CHUNKS):
        width = heads * HEAD

        def send(owner, carry):
            slot = slot_ref[owner]
            for part in range(2):
                pltpu.make_async_copy(
                    held.at[slot, :, pl.ds(part * FEATURE + start * HEAD, width)],
                    outs[number].at[owner, :, pl.ds(part * width, width)],
                    out_sem.at[number],
                ).start()
            return carry

        lax.fori_loop(0, pages, send, 0)
    for number in range(count):
        pltpu.make_async_copy(outs[number], outs[number], out_sem.at[number]).wait()


def pack(slots, pages):
    count, page_len, _ = pages.shape
    shapes = [
        jax.ShapeDtypeStruct((count, page_len, 2 * heads * HEAD), jnp.bfloat16)
        for _, heads in CHUNKS
    ]
    return pl.pallas_call(
        pack_kernel,
        out_shape=shapes,
        in_specs=[SMEM, ANY],
        out_specs=[ANY] * len(CHUNKS),
        scratch_shapes=[
            pltpu.VMEM(pages.shape, jnp.bfloat16),
            pltpu.SemaphoreType.DMA,
            pltpu.SemaphoreType.DMA((len(CHUNKS),)),
        ],
        compiler_params=pltpu.CompilerParams(vmem_limit_bytes=16 << 20),
        cost_estimate=pl.CostEstimate(flops=0, transcendentals=0, bytes_accessed=16 << 20),
        name="pack",
    )(slots, pages)


BLOCK = 4


def attend_kernel(
    start, heads, store_ref, idx_ref, arrived_ref, fresh_ref, query_ref, pick_ref, bias_ref,
    old_ref, joined_ref, part_ref, held, keys, load_sem, save_sem,
):
    width = heads * HEAD
    pages, page_len = arrived_ref.shape[:2]
    span = pages * page_len
    rows = query_ref.shape[1]
    shards = query_ref.shape[0]

    def fetch(page, carry):
        pltpu.make_async_copy(
            arrived_ref.at[store_ref[page]],
            held.at[pl.ds(pl.multiple_of(page * page_len, page_len), page_len)],
            load_sem,
        ).start()
        return carry

    lax.fori_loop(0, pages, fetch, 0)
    keys[:, HEAD:] = bias_ref[...]
    pltpu.make_async_copy(held, held, load_sem).wait()

    for row in range(rows):
        place = idx_ref[row]
        base = pl.multiple_of((place // 16) * 16, 16)
        window = held[pl.ds(base, 16), :]
        hit = lax.broadcasted_iota(jnp.int32, window.shape, 0) == place - base
        fresh = jnp.concatenate(
            [
                fresh_ref[row : row + 1, start * HEAD : start * HEAD + width],
                fresh_ref[row : row + 1, FEATURE + start * HEAD : FEATURE + start * HEAD + width],
            ],
            axis=1,
        )
        held[pl.ds(base, 16), :] = jnp.where(
            hit, fresh.astype(jnp.float32), window.astype(jnp.float32)
        ).astype(jnp.bfloat16)

    saves = []
    for part in range(2):
        save = pltpu.make_async_copy(
            held.at[:, pl.ds(part * width, width)],
            joined_ref.at[0, :, pl.ds(part * FEATURE + start * HEAD, width)],
            save_sem.at[part],
        )
        save.start()
        saves.append(save)

    lane = lax.broadcasted_iota(jnp.int32, (rows, LANES), 1)

    def split(value):
        high = value.astype(jnp.bfloat16)
        rest = value - high.astype(jnp.float32)
        middle = rest.astype(jnp.bfloat16)
        low = (rest - middle.astype(jnp.float32)).astype(jnp.bfloat16)
        return [part.astype(jnp.float32) for part in (high, middle, low)]

    for head in range(heads):
        keys[:, :HEAD] = held[:, head * HEAD : (head + 1) * HEAD]

        def block(number, carry):
            tiles = []
            for inner in range(BLOCK):
                shard = number * BLOCK + inner
                pick = pick_ref[shard]
                for group in range(GROUPS):
                    column = head * WIDE + group * HEAD
                    tiles.append(
                        jnp.concatenate(
                            [query_ref[shard, :, column : column + HEAD], pick], axis=1
                        )
                    )
            query = jnp.concatenate(tiles, axis=0)
            scores = lax.dot_general(
                query, keys[...], (((1,), (1,)), ((), ())), preferred_element_type=jnp.float32
            )
            top = jnp.maximum(jnp.max(scores, axis=1, keepdims=True), FLOOR)
            weights = jnp.exp2((scores - top) * SCALE)
            total = jnp.sum(weights, axis=1, keepdims=True)
            mixed = lax.dot_general(
                weights.astype(jnp.bfloat16),
                held[:, width + head * HEAD : width + (head + 1) * HEAD],
                (((1,), (0,)), ((), ())),
                preferred_element_type=jnp.float32,
            ).astype(jnp.bfloat16)
            for inner in range(BLOCK):
                shard = number * BLOCK + inner
                stats = jnp.zeros((rows, LANES), jnp.float32)
                tops = jnp.zeros((rows, LANES), jnp.float32)
                totals = jnp.zeros((rows, LANES), jnp.float32)
                for group in range(GROUPS):
                    first = (inner * GROUPS + group) * rows
                    column = head * WIDE + group * HEAD
                    part_ref[shard, :, column : column + HEAD] = mixed[first : first + rows]
                    mine = lane % GROUPS == group
                    tops = jnp.where(mine, top[first : first + rows], tops)
                    totals = jnp.where(mine, total[first : first + rows], totals)
                for place, piece in enumerate(split(tops) + split(totals)):
                    stats = jnp.where(lane // GROUPS == place, piece, stats)
                part_ref[shard, :, heads * WIDE + head * LANES : heads * WIDE + (head + 1) * LANES] = (
                    stats.astype(jnp.bfloat16)
                )
            return carry

        lax.fori_loop(0, shards // BLOCK, block, 0)
    for save in saves:
        save.wait()


def attend(chunk, store, idx, arrived, fresh, query, pick, bias, joined):
    start, heads = chunk
    pages, page_len, width = arrived.shape
    span = pages * page_len
    shards, rows, _ = query.shape
    operands = [store, idx, arrived, fresh, query, pick, bias]
    specs = [
        SMEM,
        SMEM,
        ANY,
        VMEM,
        pl.BlockSpec((shards, rows, heads * WIDE), lambda i: (0, 0, start // heads)),
        VMEM,
        VMEM,
    ]
    aliases = {}
    if joined is not None:
        operands.append(joined)
        specs.append(ANY)
        aliases = {len(operands) - 1: 0}
        body = functools.partial(attend_kernel, start, heads)
    else:
        def body(*refs):
            attend_kernel(start, heads, *refs[:7], None, *refs[7:])

    work = shards * rows * GROUPS * heads * span
    return pl.pallas_call(
        body,
        grid=(1,),
        out_shape=[
            jax.ShapeDtypeStruct((1, span, 2 * FEATURE), jnp.bfloat16),
            jax.ShapeDtypeStruct((shards, rows, heads * (WIDE + LANES)), jnp.bfloat16),
        ],
        in_specs=specs,
        out_specs=[ANY, VMEM],
        scratch_shapes=[
            pltpu.VMEM((span, width), jnp.bfloat16),
            pltpu.VMEM((span, 2 * HEAD), jnp.bfloat16),
            pltpu.SemaphoreType.DMA,
            pltpu.SemaphoreType.DMA((2,)),
        ],
        input_output_aliases=aliases,
        compiler_params=pltpu.CompilerParams(vmem_limit_bytes=40 << 20),
        cost_estimate=pl.CostEstimate(
            flops=work * 512, transcendentals=work, bytes_accessed=span * width * 4
        ),
        name="attend",
    )(*operands)


def merge_kernel(heads, part_ref, *refs):
    out_ref = refs[-1]
    shards, rows, _ = part_ref.shape
    for head in range(heads):
        column = heads * WIDE + head * LANES
        tops, totals = [], []
        for shard in range(shards):
            stats = part_ref[shard, :, column : column + LANES].astype(jnp.float32)
            moved = [stats] + [
                pltpu.roll(stats, LANES - GROUPS * place, 1) for place in range(1, 6)
            ]
            tops.append(moved[0] + moved[1] + moved[2])
            totals.append(moved[3] + moved[4] + moved[5])
        best = functools.reduce(jnp.maximum, tops)
        factors = [jnp.exp2((top - best) * SCALE) for top in tops]
        whole = sum(factor * total for factor, total in zip(factors, totals))
        shares = [factor / whole for factor in factors]
        for group in range(GROUPS):
            first = head * WIDE + group * HEAD
            out_ref[0, :, first : first + HEAD] = sum(
                part_ref[shard, :, first : first + HEAD].astype(jnp.float32)
                * shares[shard][:, group : group + 1]
                for shard in range(shards)
            ).astype(jnp.bfloat16)


def merge(chunk, part, attended):
    start, heads = chunk
    shards, rows, _ = part.shape
    operands, specs, aliases = [part], [VMEM], {}
    if attended is not None:
        operands.append(attended)
        specs.append(ANY)
        aliases = {1: 0}
    return pl.pallas_call(
        functools.partial(merge_kernel, heads),
        grid=(1,),
        out_shape=jax.ShapeDtypeStruct((1, rows, QHEADS * HEAD), jnp.bfloat16),
        in_specs=specs,
        out_specs=pl.BlockSpec((1, rows, heads * WIDE), lambda i: (0, 0, start // heads)),
        input_output_aliases=aliases,
        cost_estimate=pl.CostEstimate(
            flops=shards * rows * heads * WIDE * 2, transcendentals=0, bytes_accessed=1 << 20
        ),
        name="merge",
    )(*operands)


def local(
    queries, fresh_kv, cache_pages, stretch_store, stretch_request, recompute_idx, block_mask
):
    shards = lax.axis_size("ctx")
    device = lax.axis_index("ctx")
    stores = lax.axis_size("req")
    pages, page_len = cache_pages.shape[2:4]
    span = pages * page_len
    rows = queries.shape[1]
    tiles = rows // TILE

    targets = stretch_request[0, 0]
    order = jnp.arange(stores, dtype=jnp.int32)
    slots = jnp.sum(
        jnp.where(order[:, None] == targets[None, :], jnp.arange(pages, dtype=jnp.int32)[None, :], 0),
        axis=1,
        dtype=jnp.int32,
    )
    packed = pack(slots, cache_pages[0, 0])

    own_idx = lax.dynamic_index_in_dim(recompute_idx[0], device, 0, keepdims=False)
    own_pos = device * span + own_idx
    rotated = rotary(queries[0], own_pos, QHEADS).astype(jnp.bfloat16)
    query = lax.all_gather(rotated, "ctx", axis=0)
    fresh_rows = fresh_kv[0]
    fresh = jnp.concatenate(
        [rotary(fresh_rows[:, :FEATURE], own_pos, KVHEADS), fresh_rows[:, FEATURE:].astype(jnp.float32)],
        axis=1,
    ).astype(jnp.bfloat16)

    mask_cols = lax.dynamic_index_in_dim(block_mask[0], device, 2, keepdims=False) == 1
    shard_ids = jnp.arange(shards, dtype=jnp.int32)
    far = (mask_cols & (shard_ids > device)[:, None, None]).reshape(shards * tiles, pages)
    own_mask = lax.dynamic_index_in_dim(mask_cols, device, 0, keepdims=False)
    page_ids = jnp.arange(pages, dtype=jnp.int32)
    near = jnp.repeat(own_mask, TILE, axis=0) | (page_ids[None, :] == (own_idx // page_len)[:, None])
    spare = LANES - shards * tiles - rows
    allowed = jnp.concatenate([far, near, jnp.ones((spare, pages), bool)], axis=0).T
    limit = jnp.concatenate(
        [
            jnp.full((shards * tiles,), span, jnp.int32),
            own_idx,
            jnp.full((spare,), span, jnp.int32),
        ]
    )
    key_ids = jnp.arange(span, dtype=jnp.int32).reshape(pages, page_len)
    bias = jnp.where(
        allowed[:, None, :] & (key_ids[:, :, None] <= limit[None, None, :]), 0.0, NEG
    ).astype(jnp.bfloat16).reshape(span, LANES)
    row_ids = jnp.arange(rows, dtype=jnp.int32)
    column = jnp.where(
        (shard_ids == device)[:, None],
        shards * tiles + row_ids[None, :],
        shard_ids[:, None] * tiles + row_ids[None, :] // TILE,
    )
    pick = (column[:, :, None] == jnp.arange(LANES, dtype=jnp.int32)).astype(jnp.bfloat16)

    joined = attended = None
    for number, chunk in enumerate(CHUNKS):
        arrived = lax.all_to_all(packed[number], "req", split_axis=0, concat_axis=0, tiled=True)
        joined, part = attend(
            chunk, stretch_store[0, 0], own_idx, arrived, fresh, query, pick, bias, joined
        )
        part = lax.all_to_all(part, "ctx", split_axis=0, concat_axis=0, tiled=True)
        attended = merge(chunk, part, attended)
    return attended, joined


def solution(mesh):
    return jax.shard_map(
        local,
        mesh=mesh,
        in_specs=(
            P("req", "ctx", None),
            P("req", "ctx", None),
            P("req", "ctx", None, None, None),
            P("req", "ctx", None),
            P("req", "ctx", None),
            P("req", None, None),
            P("req", None, None, None, None),
        ),
        out_specs=(P("req", "ctx", None), P("req", "ctx", None)),
        check_vma=False,
    )
```

```python
import functools
import math

import jax
import jax.numpy as jnp
from jax import lax
from jax.experimental import pallas as pl
from jax.experimental.pallas import tpu as pltpu
from jax.sharding import PartitionSpec as P

QHEADS = 32
KVHEADS = 4
HEAD = 128
TILE = 8
GROUPS = QHEADS // KVHEADS
FEATURE = KVHEADS * HEAD
THETA = 500000.0
NEG = -1e30
FLOOR = -1e6
SCALE = math.log2(math.e) / math.sqrt(HEAD)
LANES = 128
WIDE = GROUPS * HEAD
CHUNKS = ((0, 2), (2, 2))
ANY = pl.BlockSpec(memory_space=pl.ANY)
VMEM = pl.BlockSpec(memory_space=pltpu.VMEM)
SMEM = pl.BlockSpec(memory_space=pltpu.SMEM)
HBM = pl.BlockSpec(memory_space=pltpu.HBM)


def rotary(values, position, head_count):
    number = values.shape[0]
    half_size = HEAD // 2
    frequency = jnp.exp(-(2.0 * jnp.arange(half_size, dtype=jnp.float32) / HEAD) * math.log(THETA))
    angles = position.astype(jnp.float32)[:, None] * frequency[None, :]
    cosine = jnp.cos(angles)[:, None, :]
    sine = jnp.sin(angles)[:, None, :]
    shaped = values.astype(jnp.float32).reshape(number, head_count, HEAD)
    first_half = shaped[..., :half_size]
    second_half = shaped[..., half_size:]
    turned = jnp.concatenate(
        [first_half * cosine - second_half * sine, second_half * cosine + first_half * sine],
        axis=-1,
    )
    return turned.reshape(number, head_count * HEAD)


def ways(chunk):
    start, heads = chunk
    width = heads * HEAD
    return ((start * HEAD, width, 0), (FEATURE + start * HEAD, width, width))


def pack_kernel(chunk, slot_ref, pages_ref, out_ref, held, in_sem, out_sem):
    loads, saves = [], []
    for owner in range(pages_ref.shape[0]):
        for half, (start, width, column) in enumerate(ways(chunk)):
            load = pltpu.make_async_copy(
                pages_ref.at[slot_ref[owner], :, pl.ds(start, width)],
                held.at[owner, :, pl.ds(column, width)],
                in_sem.at[owner, half],
            )
            load.start()
            loads.append(load)
    for owner in range(pages_ref.shape[0]):
        loads[2 * owner].wait()
        loads[2 * owner + 1].wait()
        save = pltpu.make_async_copy(held.at[owner], out_ref.at[owner], out_sem.at[owner])
        save.start()
        saves.append(save)
    for save in saves:
        save.wait()


def pack(name, chunk, slots, pages):
    count, page_len, _ = pages.shape
    shape = (count, page_len, 2 * chunk[1] * HEAD)
    return pl.pallas_call(
        functools.partial(pack_kernel, chunk),
        out_shape=jax.ShapeDtypeStruct(shape, jnp.bfloat16),
        in_specs=[SMEM, HBM],
        out_specs=HBM,
        scratch_shapes=[
            pltpu.VMEM(shape, jnp.bfloat16),
            pltpu.SemaphoreType.DMA((count, 2)),
            pltpu.SemaphoreType.DMA((count,)),
        ],
        compiler_params=pltpu.CompilerParams(vmem_limit_bytes=60 << 20),
        cost_estimate=pl.CostEstimate(flops=0, transcendentals=0, bytes_accessed=8 << 20),
        name=name,
    )(slots, pages)


BLOCK = 2
KB = 512


def attend_kernel(
    start, heads, held_back, count, place_ref, order_ref, from_ref, idx_ref, fresh_ref,
    query_ref, pick_ref, bias_ref, *refs,
):
    arrived_ref, refs = refs[0], refs[held_back:]
    joined_ref, parts, (held, keys, scores_s, probs_s, load_sem, save_sem) = (
        refs[0], refs[1 : 1 + count], refs[1 + count :],
    )
    width = heads * HEAD
    span = bias_ref.shape[0]
    pages, page_len = arrived_ref.shape[:2]
    rows = query_ref.shape[1]
    shards = query_ref.shape[0]
    if count == 1:
        parts = [parts[0].at[shard] for shard in range(shards)]

    for source in range(pages):
        place = pl.ds(pl.multiple_of(place_ref[source] * page_len, page_len), page_len)
        pltpu.make_async_copy(arrived_ref.at[source], held.at[place], load_sem).start()
    keys[:, HEAD:] = bias_ref[...]
    pltpu.make_async_copy(held, held, load_sem).wait()

    for row in range(rows):
        place = idx_ref[row]
        base = pl.multiple_of((place // 16) * 16, 16)
        window = held[pl.ds(base, 16), :]
        hit = lax.broadcasted_iota(jnp.int32, window.shape, 0) == place - base
        fresh = jnp.concatenate(
            [
                fresh_ref[row : row + 1, start * HEAD : start * HEAD + width],
                fresh_ref[row : row + 1, FEATURE + start * HEAD : FEATURE + start * HEAD + width],
            ],
            axis=1,
        )
        held[pl.ds(base, 16), :] = jnp.where(
            hit, fresh.astype(jnp.float32), window.astype(jnp.float32)
        ).astype(jnp.bfloat16)

    saves = []
    for part in range(2):
        save = pltpu.make_async_copy(
            held.at[:, pl.ds(part * width, width)],
            joined_ref.at[0, :, pl.ds(part * FEATURE + start * HEAD, width)],
            save_sem.at[part],
        )
        save.start()
        saves.append(save)

    lane = lax.broadcasted_iota(jnp.int32, (rows, LANES), 1)

    def split(value):
        high = value.astype(jnp.bfloat16)
        rest = value - high.astype(jnp.float32)
        middle = rest.astype(jnp.bfloat16)
        low = (rest - middle.astype(jnp.float32)).astype(jnp.bfloat16)
        return [part.astype(jnp.float32) for part in (high, middle, low)]

    span_blocks = span // KB
    def lanes(start, size):
        return pl.ds(start if isinstance(start, int) else pl.multiple_of(start, LANES), size)

    def one_head(head, carry):
        keys[:, :HEAD] = held[:, lanes(head * HEAD, HEAD)]

        def first(number, slot):
            tiles = []
            for inner in range(BLOCK):
                shard = from_ref[number * BLOCK + inner]
                pick = pick_ref[order_ref[number * BLOCK + inner]]
                for group in range(GROUPS):
                    column = head * WIDE + group * HEAD
                    tiles.append(
                        jnp.concatenate(
                            [query_ref[shard, :, lanes(column, HEAD)], pick], axis=1
                        )
                    )
            query = jnp.concatenate(tiles, axis=0)
            top = None
            for kb in range(span_blocks):
                s = lax.dot_general(
                    query, keys[kb * KB : (kb + 1) * KB], (((1,), (1,)), ((), ())),
                    preferred_element_type=jnp.float32,
                )
                scores_s[slot, :, kb * KB : (kb + 1) * KB] = s
                for c in range(KB // LANES):
                    t = s[:, c * LANES : (c + 1) * LANES]
                    top = t if top is None else jnp.maximum(top, t)
            return jnp.maximum(jnp.max(top, axis=1, keepdims=True), FLOOR)

        def second(number, slot, top):
            total = None
            for c in range(span // LANES):
                p = jnp.exp2((scores_s[slot, :, c * LANES : (c + 1) * LANES] - top) * SCALE)
                total = p if total is None else total + p
                probs_s[slot, :, c * LANES : (c + 1) * LANES] = p.astype(jnp.bfloat16)
            total = jnp.sum(total, axis=1, keepdims=True)
            mixed = lax.dot_general(
                probs_s[slot],
                held[:, lanes(width + head * HEAD, HEAD)],
                (((1,), (0,)), ((), ())),
                preferred_element_type=jnp.float32,
            ).astype(jnp.bfloat16)
            for inner in range(BLOCK):
                shard = number * BLOCK + inner
                stats = jnp.zeros((rows, LANES), jnp.float32)
                tops = jnp.zeros((rows, LANES), jnp.float32)
                totals = jnp.zeros((rows, LANES), jnp.float32)
                for group in range(GROUPS):
                    first = (inner * GROUPS + group) * rows
                    column = head * WIDE + group * HEAD
                    parts[shard][:, lanes(column, HEAD)] = mixed[first : first + rows]
                    mine = lane % GROUPS == group
                    tops = jnp.where(mine, top[first : first + rows], tops)
                    totals = jnp.where(mine, total[first : first + rows], totals)
                for place, piece in enumerate(split(tops) + split(totals)):
                    stats = jnp.where(lane // GROUPS == place, piece, stats)
                parts[shard][:, lanes(heads * WIDE + head * LANES, LANES)] = (
                    stats.astype(jnp.bfloat16)
                )

        count = shards // BLOCK
        top = first(0, 0)
        for number in range(count):
            after = first(number + 1, (number + 1) % 2) if number + 1 < count else None
            second(number, number % 2, top)
            top = after
        return carry

    if count == 1:
        for head in range(heads):
            one_head(head, 0)
    else:
        lax.fori_loop(0, heads, one_head, 0)
    for save in saves:
        save.wait()


def attend(chunk, count, tables, arrived, fresh, query, pick, bias, joined, after=()):
    start, heads = chunk
    width = 2 * heads * HEAD
    span = bias.shape[0]
    shards, rows, _ = query.shape
    operands = list(tables) + [fresh, query, pick, bias, arrived]
    specs = [SMEM] * len(tables) + [
        VMEM,
        pl.BlockSpec((shards, rows, heads * WIDE), lambda i: (0, 0, start // heads)),
        VMEM,
        VMEM,
        HBM,
    ]
    aliases = {}
    if joined is not None:
        operands.append(joined)
        specs.append(HBM)
        aliases = {len(operands) - 1: 0}
    operands += after
    specs += [HBM] * len(after)
    across = heads * (WIDE + LANES)
    part = (rows, across) if count > 1 else (shards, rows, across)
    work = shards * rows * GROUPS * heads * span
    return pl.pallas_call(
        functools.partial(attend_kernel, start, heads, len(operands) - len(tables) - 4, count),
        grid=(1,),
        out_shape=[
            jax.ShapeDtypeStruct((1, span, 2 * FEATURE), jnp.bfloat16),
        ]
        + [jax.ShapeDtypeStruct(part, jnp.bfloat16)] * count,
        in_specs=specs,
        out_specs=[HBM] + [VMEM] * count,
        scratch_shapes=[
            pltpu.VMEM((span, width), jnp.bfloat16),
            pltpu.VMEM((span, 2 * HEAD), jnp.bfloat16),
            pltpu.VMEM((2, BLOCK * LANES, span), jnp.float32),
            pltpu.VMEM((2, BLOCK * LANES, span), jnp.bfloat16),
            pltpu.SemaphoreType.DMA,
            pltpu.SemaphoreType.DMA((2,)),
        ],
        input_output_aliases=aliases,
        compiler_params=pltpu.CompilerParams(vmem_limit_bytes=60 << 20),
        cost_estimate=pl.CostEstimate(
            flops=work * 5120, transcendentals=work, bytes_accessed=span * width * 4
        ),
        name="attend",
    )(*operands)


def merge_kernel(heads, count, *refs):
    parts, out_ref = refs[:count], refs[-1]
    if count == 1:
        parts = [parts[0].at[shard] for shard in range(parts[0].shape[0])]
    shards = len(parts)
    for head in range(heads):
        column = heads * WIDE + head * LANES
        tops, totals = [], []
        for shard in range(shards):
            stats = parts[shard][:, column : column + LANES].astype(jnp.float32)
            moved = [stats] + [
                pltpu.roll(stats, LANES - GROUPS * place, 1) for place in range(1, 6)
            ]
            tops.append(moved[0] + moved[1] + moved[2])
            totals.append(moved[3] + moved[4] + moved[5])
        best = functools.reduce(jnp.maximum, tops)
        factors = [jnp.exp2((top - best) * SCALE) for top in tops]
        whole = sum(factor * total for factor, total in zip(factors, totals))
        shares = [factor / whole for factor in factors]
        for group in range(GROUPS):
            first = head * WIDE + group * HEAD
            out_ref[0, :, first : first + HEAD] = sum(
                parts[shard][:, first : first + HEAD].astype(jnp.float32)
                * shares[shard][:, group : group + 1]
                for shard in range(shards)
            ).astype(jnp.bfloat16)


def merge(chunk, parts, attended):
    start, heads = chunk
    rows = parts[0].shape[-2]
    operands, specs, aliases = list(parts), [VMEM] * len(parts), {}
    if attended is not None:
        operands.append(attended)
        specs.append(HBM)
        aliases = {len(operands) - 1: 0}
    return pl.pallas_call(
        functools.partial(merge_kernel, heads, len(parts)),
        grid=(1,),
        out_shape=jax.ShapeDtypeStruct((1, rows, QHEADS * HEAD), jnp.bfloat16),
        in_specs=specs,
        out_specs=pl.BlockSpec((1, rows, heads * WIDE), lambda i: (0, 0, start // heads)),
        input_output_aliases=aliases,
        cost_estimate=pl.CostEstimate(
            flops=rows * heads * WIDE * 16, transcendentals=0, bytes_accessed=1 << 20
        ),
        name="merge",
    )(*operands)


def local(
    queries, fresh_kv, cache_pages, stretch_store, stretch_request, recompute_idx, block_mask
):
    shards = lax.axis_size("ctx")
    device = lax.axis_index("ctx")
    stores = lax.axis_size("req")
    pages, page_len = cache_pages.shape[2:4]
    span = pages * page_len
    rows = queries.shape[1]
    tiles = rows // TILE

    order = jnp.arange(stores, dtype=jnp.int32)

    def find(table):
        return jnp.sum(jnp.where(order[:, None] == table[None, :], order[None, :], 0), axis=1, dtype=jnp.int32)

    first, last = CHUNKS
    slots = find(stretch_request[0, 0])
    places = find(stretch_store[0, 0])
    store = cache_pages[0, 0]
    early = lax.all_to_all(
        pack("pack", first, slots, store), "req", split_axis=0, concat_axis=0, tiled=True
    )
    late = lax.all_to_all(
        pack("pack_rest", last, slots, store), "req", split_axis=0, concat_axis=0, tiled=True
    )

    own_idx = lax.dynamic_index_in_dim(recompute_idx[0], device, 0, keepdims=False)
    own_pos = device * span + own_idx
    rotated = rotary(queries[0], own_pos, QHEADS).astype(jnp.bfloat16)
    twin = lax.ppermute(rotated, "ctx", [(i, i ^ 1) for i in range(shards)])
    pair = jnp.stack([rotated, twin])
    query = jnp.concatenate(
        [pair]
        + [
            lax.ppermute(pair, "ctx", [(i, (i + 2 * s) % shards) for i in range(shards)])
            for s in range(1, shards // 2)
        ]
    )

    def slot_of(shard):
        odd = (shard ^ device) & 1
        return (device - (shard ^ odd)) % shards + odd

    fresh_rows = fresh_kv[0]
    fresh = jnp.concatenate(
        [rotary(fresh_rows[:, :FEATURE], own_pos, KVHEADS), fresh_rows[:, FEATURE:].astype(jnp.float32)],
        axis=1,
    ).astype(jnp.bfloat16)

    mask_cols = lax.dynamic_index_in_dim(block_mask[0], device, 2, keepdims=False) == 1
    shard_ids = jnp.arange(shards, dtype=jnp.int32)
    far = (mask_cols & (shard_ids > device)[:, None, None]).reshape(shards * tiles, pages)
    own_mask = lax.dynamic_index_in_dim(mask_cols, device, 0, keepdims=False)
    page_ids = jnp.arange(pages, dtype=jnp.int32)
    near = jnp.repeat(own_mask, TILE, axis=0) | (page_ids[None, :] == (own_idx // page_len)[:, None])
    spare = LANES - shards * tiles - rows
    allowed = jnp.concatenate([far, near, jnp.ones((spare, pages), bool)], axis=0).T
    limit = jnp.concatenate(
        [
            jnp.full((shards * tiles,), span, jnp.int32),
            own_idx,
            jnp.full((spare,), span, jnp.int32),
        ]
    )
    key_ids = jnp.arange(span, dtype=jnp.int32).reshape(pages, page_len)
    bias = jnp.where(
        allowed[:, None, :] & (key_ids[:, :, None] <= limit[None, None, :]), 0.0, NEG
    ).astype(jnp.bfloat16).reshape(span, LANES)
    row_ids = jnp.arange(rows, dtype=jnp.int32)
    column = jnp.where(
        (shard_ids == device)[:, None],
        shards * tiles + row_ids[None, :],
        shard_ids[:, None] * tiles + row_ids[None, :] // TILE,
    )
    pick = (column[:, :, None] == jnp.arange(LANES, dtype=jnp.int32)).astype(jnp.bfloat16)

    turn = (device + shard_ids) % shards
    joined, *parts = attend(
        first, shards, (places, turn, slot_of(turn), own_idx), early, fresh, query, pick, bias, None
    )
    parts = [parts[0]] + [
        lax.ppermute(parts[s], "ctx", [(i, (i + s) % shards) for i in range(shards)])
        for s in range(1, shards)
    ]
    attended = merge(first, parts, None)
    joined, part = attend(
        last, 1, (places, shard_ids, slot_of(shard_ids), own_idx), late, fresh, query, pick, bias, joined, [attended]
    )
    part = lax.all_to_all(part, "ctx", split_axis=0, concat_axis=0, tiled=True)
    attended = merge(last, [part], attended)
    return attended, joined


def solution(mesh):
    return jax.shard_map(
        local,
        mesh=mesh,
        in_specs=(
            P("req", "ctx", None),
            P("req", "ctx", None),
            P("req", "ctx", None, None, None),
            P("req", "ctx", None),
            P("req", "ctx", None),
            P("req", None, None),
            P("req", None, None, None, None),
        ),
        out_specs=(P("req", "ctx", None), P("req", "ctx", None)),
        check_vma=False,
    )
```

```python
import functools
import math

import jax
import jax.numpy as jnp
from jax import lax
from jax.experimental import pallas as pl
from jax.experimental.pallas import tpu as pltpu
from jax.sharding import PartitionSpec as P

QHEADS = 32
KVHEADS = 4
HEAD = 128
TILE = 8
GROUPS = QHEADS // KVHEADS
FEATURE = KVHEADS * HEAD
THETA = 500000.0
NEG = -1e30
FLOOR = -1e6
SCALE = math.log2(math.e) / math.sqrt(HEAD)
LANES = 128
WIDE = GROUPS * HEAD
CHUNKS = ((0, 2), (2, 2))
ANY = pl.BlockSpec(memory_space=pl.ANY)
VMEM = pl.BlockSpec(memory_space=pltpu.VMEM)
SMEM = pl.BlockSpec(memory_space=pltpu.SMEM)
HBM = pl.BlockSpec(memory_space=pltpu.HBM)


def rotary(values, position, head_count):
    number = values.shape[0]
    half_size = HEAD // 2
    frequency = jnp.exp(-(2.0 * jnp.arange(half_size, dtype=jnp.float32) / HEAD) * math.log(THETA))
    angles = position.astype(jnp.float32)[:, None] * frequency[None, :]
    cosine = jnp.cos(angles)[:, None, :]
    sine = jnp.sin(angles)[:, None, :]
    shaped = values.astype(jnp.float32).reshape(number, head_count, HEAD)
    first_half = shaped[..., :half_size]
    second_half = shaped[..., half_size:]
    turned = jnp.concatenate(
        [first_half * cosine - second_half * sine, second_half * cosine + first_half * sine],
        axis=-1,
    )
    return turned.reshape(number, head_count * HEAD)


def ways(chunk):
    start, heads = chunk
    width = heads * HEAD
    return ((start * HEAD, width, 0), (FEATURE + start * HEAD, width, width))


def pack_kernel(chunk, owner_ref, pages_ref, out_ref, held, in_sem, out_sem):
    loads, saves = [], []
    for slot in range(pages_ref.shape[0]):
        for half, (start, width, column) in enumerate(ways(chunk)):
            load = pltpu.make_async_copy(
                pages_ref.at[slot, :, pl.ds(start, width)],
                held.at[slot, :, pl.ds(column, width)],
                in_sem.at[slot, half],
            )
            load.start()
            loads.append(load)
    for slot in range(pages_ref.shape[0]):
        loads[2 * slot].wait()
        loads[2 * slot + 1].wait()
        save = pltpu.make_async_copy(held.at[slot], out_ref.at[owner_ref[slot]], out_sem.at[slot])
        save.start()
        saves.append(save)
    for save in saves:
        save.wait()


def pack(name, chunk, owners, pages):
    count, page_len, _ = pages.shape
    shape = (count, page_len, 2 * chunk[1] * HEAD)
    return pl.pallas_call(
        functools.partial(pack_kernel, chunk),
        out_shape=jax.ShapeDtypeStruct(shape, jnp.bfloat16),
        in_specs=[SMEM, HBM],
        out_specs=HBM,
        scratch_shapes=[
            pltpu.VMEM(shape, jnp.bfloat16),
            pltpu.SemaphoreType.DMA((count, 2)),
            pltpu.SemaphoreType.DMA((count,)),
        ],
        compiler_params=pltpu.CompilerParams(vmem_limit_bytes=60 << 20),
        cost_estimate=pl.CostEstimate(flops=0, transcendentals=0, bytes_accessed=8 << 20),
        name=name,
    )(owners, pages)


BLOCK = 2
KB = 512


def attend_kernel(
    start, heads, held_back, count, store_ref, order_ref, from_ref, idx_ref, fresh_ref,
    query_ref, pick_ref, bias_ref, *refs,
):
    arrived_ref, refs = refs[0], refs[held_back:]
    joined_ref, parts, (held, keys, scores_s, probs_s, load_sem, save_sem) = (
        refs[0], refs[1 : 1 + count], refs[1 + count :],
    )
    width = heads * HEAD
    span = bias_ref.shape[0]
    pages, page_len = arrived_ref.shape[:2]
    rows = query_ref.shape[1]
    shards = query_ref.shape[0]
    if count == 1:
        parts = [parts[0].at[shard] for shard in range(shards)]

    for page in range(pages):
        place = pl.ds(page * page_len, page_len)
        pltpu.make_async_copy(arrived_ref.at[store_ref[page]], held.at[place], load_sem).start()
    keys[:, HEAD:] = bias_ref[...]
    pltpu.make_async_copy(held, held, load_sem).wait()

    for row in range(rows):
        place = idx_ref[row]
        base = pl.multiple_of((place // 16) * 16, 16)
        window = held[pl.ds(base, 16), :]
        hit = lax.broadcasted_iota(jnp.int32, window.shape, 0) == place - base
        fresh = jnp.concatenate(
            [
                fresh_ref[row : row + 1, start * HEAD : start * HEAD + width],
                fresh_ref[row : row + 1, FEATURE + start * HEAD : FEATURE + start * HEAD + width],
            ],
            axis=1,
        )
        held[pl.ds(base, 16), :] = jnp.where(
            hit, fresh.astype(jnp.float32), window.astype(jnp.float32)
        ).astype(jnp.bfloat16)

    saves = []
    for part in range(2):
        save = pltpu.make_async_copy(
            held.at[:, pl.ds(part * width, width)],
            joined_ref.at[0, :, pl.ds(part * FEATURE + start * HEAD, width)],
            save_sem.at[part],
        )
        save.start()
        saves.append(save)

    lane = lax.broadcasted_iota(jnp.int32, (rows, LANES), 1)

    def split(value):
        high = value.astype(jnp.bfloat16)
        rest = value - high.astype(jnp.float32)
        middle = rest.astype(jnp.bfloat16)
        low = (rest - middle.astype(jnp.float32)).astype(jnp.bfloat16)
        return [part.astype(jnp.float32) for part in (high, middle, low)]

    span_blocks = span // KB
    def lanes(start, size):
        return pl.ds(start if isinstance(start, int) else pl.multiple_of(start, LANES), size)

    def one_head(head, carry):
        keys[:, :HEAD] = held[:, lanes(head * HEAD, HEAD)]

        def first(number, slot):
            tiles = []
            for inner in range(BLOCK):
                shard = from_ref[number * BLOCK + inner]
                pick = pick_ref[order_ref[number * BLOCK + inner]]
                for group in range(GROUPS):
                    column = head * WIDE + group * HEAD
                    tiles.append(
                        jnp.concatenate(
                            [query_ref[shard, :, lanes(column, HEAD)], pick], axis=1
                        )
                    )
            query = jnp.concatenate(tiles, axis=0)
            top = None
            for kb in range(span_blocks):
                s = lax.dot_general(
                    query, keys[kb * KB : (kb + 1) * KB], (((1,), (1,)), ((), ())),
                    preferred_element_type=jnp.float32,
                )
                scores_s[slot, :, kb * KB : (kb + 1) * KB] = s
                for c in range(KB // LANES):
                    t = s[:, c * LANES : (c + 1) * LANES]
                    top = t if top is None else jnp.maximum(top, t)
            return jnp.maximum(jnp.max(top, axis=1, keepdims=True), FLOOR)

        def second(number, slot, top):
            total = None
            for c in range(span // LANES):
                p = jnp.exp2((scores_s[slot, :, c * LANES : (c + 1) * LANES] - top) * SCALE)
                total = p if total is None else total + p
                probs_s[slot, :, c * LANES : (c + 1) * LANES] = p.astype(jnp.bfloat16)
            total = jnp.sum(total, axis=1, keepdims=True)
            mixed = lax.dot_general(
                probs_s[slot],
                held[:, lanes(width + head * HEAD, HEAD)],
                (((1,), (0,)), ((), ())),
                preferred_element_type=jnp.float32,
            ).astype(jnp.bfloat16)
            for inner in range(BLOCK):
                shard = number * BLOCK + inner
                stats = jnp.zeros((rows, LANES), jnp.float32)
                tops = jnp.zeros((rows, LANES), jnp.float32)
                totals = jnp.zeros((rows, LANES), jnp.float32)
                for group in range(GROUPS):
                    first = (inner * GROUPS + group) * rows
                    column = head * WIDE + group * HEAD
                    parts[shard][:, lanes(column, HEAD)] = mixed[first : first + rows]
                    mine = lane % GROUPS == group
                    tops = jnp.where(mine, top[first : first + rows], tops)
                    totals = jnp.where(mine, total[first : first + rows], totals)
                for place, piece in enumerate(split(tops) + split(totals)):
                    stats = jnp.where(lane // GROUPS == place, piece, stats)
                parts[shard][:, lanes(heads * WIDE + head * LANES, LANES)] = (
                    stats.astype(jnp.bfloat16)
                )

        count = shards // BLOCK
        top = first(0, 0)
        for number in range(count):
            after = first(number + 1, (number + 1) % 2) if number + 1 < count else None
            second(number, number % 2, top)
            top = after
        return carry

    if count == 1:
        for head in range(heads):
            one_head(head, 0)
    else:
        lax.fori_loop(0, heads, one_head, 0)
    for save in saves:
        save.wait()


def attend(chunk, count, tables, arrived, fresh, query, pick, bias, joined, after=()):
    start, heads = chunk
    width = 2 * heads * HEAD
    span = bias.shape[0]
    shards, rows, _ = query.shape
    operands = list(tables) + [fresh, query, pick, bias, arrived]
    specs = [SMEM] * len(tables) + [
        VMEM,
        pl.BlockSpec((shards, rows, heads * WIDE), lambda i: (0, 0, start // heads)),
        VMEM,
        VMEM,
        HBM,
    ]
    aliases = {}
    if joined is not None:
        operands.append(joined)
        specs.append(HBM)
        aliases = {len(operands) - 1: 0}
    operands += after
    specs += [HBM] * len(after)
    across = heads * (WIDE + LANES)
    part = (rows, across) if count > 1 else (shards, rows, across)
    work = shards * rows * GROUPS * heads * span
    return pl.pallas_call(
        functools.partial(attend_kernel, start, heads, len(operands) - len(tables) - 4, count),
        grid=(1,),
        out_shape=[
            jax.ShapeDtypeStruct((1, span, 2 * FEATURE), jnp.bfloat16),
        ]
        + [jax.ShapeDtypeStruct(part, jnp.bfloat16)] * count,
        in_specs=specs,
        out_specs=[HBM] + [VMEM] * count,
        scratch_shapes=[
            pltpu.VMEM((span, width), jnp.bfloat16),
            pltpu.VMEM((span, 2 * HEAD), jnp.bfloat16),
            pltpu.VMEM((2, BLOCK * LANES, span), jnp.float32),
            pltpu.VMEM((2, BLOCK * LANES, span), jnp.bfloat16),
            pltpu.SemaphoreType.DMA,
            pltpu.SemaphoreType.DMA((2,)),
        ],
        input_output_aliases=aliases,
        compiler_params=pltpu.CompilerParams(vmem_limit_bytes=60 << 20),
        cost_estimate=pl.CostEstimate(
            flops=work * 5120, transcendentals=work, bytes_accessed=span * width * 4
        ),
        name="attend",
    )(*operands)


def merge_kernel(heads, count, *refs):
    parts, out_ref = refs[:count], refs[-1]
    if count == 1:
        parts = [parts[0].at[shard] for shard in range(parts[0].shape[0])]
    shards = len(parts)
    for head in range(heads):
        column = heads * WIDE + head * LANES
        tops, totals = [], []
        for shard in range(shards):
            stats = parts[shard][:, column : column + LANES].astype(jnp.float32)
            moved = [stats] + [
                pltpu.roll(stats, LANES - GROUPS * place, 1) for place in range(1, 6)
            ]
            tops.append(moved[0] + moved[1] + moved[2])
            totals.append(moved[3] + moved[4] + moved[5])
        best = functools.reduce(jnp.maximum, tops)
        factors = [jnp.exp2((top - best) * SCALE) for top in tops]
        whole = sum(factor * total for factor, total in zip(factors, totals))
        shares = [factor / whole for factor in factors]
        for group in range(GROUPS):
            first = head * WIDE + group * HEAD
            out_ref[0, :, first : first + HEAD] = sum(
                parts[shard][:, first : first + HEAD].astype(jnp.float32)
                * shares[shard][:, group : group + 1]
                for shard in range(shards)
            ).astype(jnp.bfloat16)


def merge(chunk, parts, attended):
    start, heads = chunk
    rows = parts[0].shape[-2]
    operands, specs, aliases = list(parts), [VMEM] * len(parts), {}
    if attended is not None:
        operands.append(attended)
        specs.append(HBM)
        aliases = {len(operands) - 1: 0}
    return pl.pallas_call(
        functools.partial(merge_kernel, heads, len(parts)),
        grid=(1,),
        out_shape=jax.ShapeDtypeStruct((1, rows, QHEADS * HEAD), jnp.bfloat16),
        in_specs=specs,
        out_specs=pl.BlockSpec((1, rows, heads * WIDE), lambda i: (0, 0, start // heads)),
        input_output_aliases=aliases,
        cost_estimate=pl.CostEstimate(
            flops=rows * heads * WIDE * 16, transcendentals=0, bytes_accessed=1 << 20
        ),
        name="merge",
    )(*operands)


def local(
    queries, fresh_kv, cache_pages, stretch_store, stretch_request, recompute_idx, block_mask
):
    shards = lax.axis_size("ctx")
    device = lax.axis_index("ctx")
    pages, page_len = cache_pages.shape[2:4]
    span = pages * page_len
    rows = queries.shape[1]
    tiles = rows // TILE

    first, last = CHUNKS
    owners = stretch_request[0, 0]
    places = stretch_store[0, 0]
    store = cache_pages[0, 0]
    early = lax.all_to_all(
        pack("pack", first, owners, store), "req", split_axis=0, concat_axis=0, tiled=True
    )
    late = lax.all_to_all(
        pack("pack_rest", last, owners, store), "req", split_axis=0, concat_axis=0, tiled=True
    )

    own_idx = lax.dynamic_index_in_dim(recompute_idx[0], device, 0, keepdims=False)
    own_pos = device * span + own_idx
    rotated = rotary(queries[0], own_pos, QHEADS).astype(jnp.bfloat16)
    twin = lax.ppermute(rotated, "ctx", [(i, i ^ 1) for i in range(shards)])
    pair = jnp.stack([rotated, twin])
    query = jnp.concatenate(
        [pair]
        + [
            lax.ppermute(pair, "ctx", [(i, (i + 2 * s) % shards) for i in range(shards)])
            for s in range(1, shards // 2)
        ]
    )

    def slot_of(shard):
        odd = (shard ^ device) & 1
        return (device - (shard ^ odd)) % shards + odd

    fresh_rows = fresh_kv[0]
    fresh = jnp.concatenate(
        [rotary(fresh_rows[:, :FEATURE], own_pos, KVHEADS), fresh_rows[:, FEATURE:].astype(jnp.float32)],
        axis=1,
    ).astype(jnp.bfloat16)

    mask_cols = lax.dynamic_index_in_dim(block_mask[0], device, 2, keepdims=False) == 1
    shard_ids = jnp.arange(shards, dtype=jnp.int32)
    far = (mask_cols & (shard_ids > device)[:, None, None]).reshape(shards * tiles, pages)
    own_mask = lax.dynamic_index_in_dim(mask_cols, device, 0, keepdims=False)
    page_ids = jnp.arange(pages, dtype=jnp.int32)
    near = jnp.repeat(own_mask, TILE, axis=0) | (page_ids[None, :] == (own_idx // page_len)[:, None])
    spare = LANES - shards * tiles - rows
    allowed = jnp.concatenate([far, near, jnp.ones((spare, pages), bool)], axis=0).T
    limit = jnp.concatenate(
        [
            jnp.full((shards * tiles,), span, jnp.int32),
            own_idx,
            jnp.full((spare,), span, jnp.int32),
        ]
    )
    key_ids = jnp.arange(span, dtype=jnp.int32).reshape(pages, page_len)
    bias = jnp.where(
        allowed[:, None, :] & (key_ids[:, :, None] <= limit[None, None, :]), 0.0, NEG
    ).astype(jnp.bfloat16).reshape(span, LANES)
    row_ids = jnp.arange(rows, dtype=jnp.int32)
    column = jnp.where(
        (shard_ids == device)[:, None],
        shards * tiles + row_ids[None, :],
        shard_ids[:, None] * tiles + row_ids[None, :] // TILE,
    )
    pick = (column[:, :, None] == jnp.arange(LANES, dtype=jnp.int32)).astype(jnp.bfloat16)

    turn = (device + shard_ids) % shards
    joined, *parts = attend(
        first, shards, (places, turn, slot_of(turn), own_idx), early, fresh, query, pick, bias, None
    )
    parts = [parts[0]] + [
        lax.ppermute(parts[s], "ctx", [(i, (i + s) % shards) for i in range(shards)])
        for s in range(1, shards)
    ]
    attended = merge(first, parts, None)
    joined, part = attend(
        last, 1, (places, shard_ids, slot_of(shard_ids), own_idx), late, fresh, query, pick, bias, joined, [attended]
    )
    part = lax.all_to_all(part, "ctx", split_axis=0, concat_axis=0, tiled=True)
    attended = merge(last, [part], attended)
    return attended, joined


def solution(mesh):
    return jax.shard_map(
        local,
        mesh=mesh,
        in_specs=(
            P("req", "ctx", None),
            P("req", "ctx", None),
            P("req", "ctx", None, None, None),
            P("req", "ctx", None),
            P("req", "ctx", None),
            P("req", None, None),
            P("req", None, None, None, None),
        ),
        out_specs=(P("req", "ctx", None), P("req", "ctx", None)),
        check_vma=False,
    )
```
